512 devices in a mesh: area: 8 (over y), hor: 16 (over z, core), scen: 4 (over x).
Axes of the slice: x: 4, y: 8, z: 8, core: 2. Of those that a mesh axis runs over, the one named last changes fastest.
Arguments:
- diagonal: float32 [8, 32, 384], P('area', 'hor'), may hold values from 0.25 to 1
- band_coef: float32 [8, 32, 4, 384], P('area', 'hor'), may hold values from -0.1 to 0.1
- band_offsets: int32 [8, 4], P('area'), may hold values from -16 to 16, as said below
- boundary_index: int32 [8, 128], P('area'), may hold values from 0 to 383, as said below
- adjacency: int32 [8, 3], P('area'), may hold values from 0 to 7, as said below
- start_state: float32 [8, 384], P('area'), may hold values from -6 to 6
- input_matrix: float32 [8, 384, 128], P('area'), may hold values from -0.3125 to 0.3125
- input_penalty: float32 [8, 128], P('area'), may hold values from 0.5 to 2
- linear_cost: float32 [8, 32, 64, 384], P('area', 'hor', 'scen'), may hold values from -1.2 to 1.2
- disturbance: float32 [8, 32, 64, 384], P('area', 'hor', 'scen'), may hold values from -0.6 to 0.6
- consensus: float32 [8, 32, 64, 128], P('area', 'hor', 'scen'), may hold values from -1.8 to 1.8
- dual_values: float32 [8, 32, 64, 128], P('area', 'hor', 'scen'), may hold values from -1.8 to 1.8
Outputs:
- trajectory: float32 [8, 32, 64, 384], P('area', 'hor', 'scen')
- agreed_boundary: float32 [8, 32, 64, 128], P('area', 'hor', 'scen')
- updated_duals: float32 [8, 32, 64, 128], P('area', 'hor', 'scen')
The draws below stay inside these ranges and needn't reach their ends.
Inputs may be any that keep to these rules, and one draw needn't show every extreme that they name: `band_offsets`: every entry is 16 or -16; the first two entries of every row are 16 and -16. `boundary_index`: the entries of a row are distinct, and every row holds 0 and 383. `adjacency`: the first entry of row a differs from a; the other entries may repeat and may equal a.
All inputs are finite; a program needn't handle non-finite values.
Results may differ from the reference program's by a relative error of at most 0.0003.
Values sent between devices are 32-bit elements; how exact they have to be, the bound alone decides.
A program may use at most 64 MiB of HBM per device.

```python
import math
import jax
import jax.numpy as jnp
from jax import lax

AREA_STATES = 384
NU = 128
NBD = 128
NB = 4
MAXOFF = 16
NNB = 3
SECTION_DEV = 2
GRID_AREAS = 8
HORIZON_SECTIONS = 32
SCENS = 64


def draw_diagonal(key, part):
    random_keys = jax.random.split(key, 6)
    share = 0.5
    slow = jax.random.uniform(random_keys[0], (GRID_AREAS, 1, AREA_STATES)) < share
    slow_rate = math.log(10.0) / HORIZON_SECTIONS * jax.random.uniform(random_keys[1], (GRID_AREAS, 1, AREA_STATES), minval=0.05, maxval=0.2)
    fast_rate = jnp.exp(jax.random.uniform(random_keys[2], (GRID_AREAS, 1, AREA_STATES), minval=math.log(0.03), maxval=math.log(0.3)))
    segments = HORIZON_SECTIONS // SECTION_DEV
    factor = jnp.exp(jax.random.uniform(random_keys[3], (GRID_AREAS, segments, 1, AREA_STATES), minval=math.log(0.5), maxval=math.log(2.0)))
    factor = jnp.broadcast_to(factor, (GRID_AREAS, segments, SECTION_DEV, AREA_STATES)).reshape(GRID_AREAS, HORIZON_SECTIONS, AREA_STATES)
    decay_rate = jnp.where(slow, slow_rate, fast_rate) * factor
    outage_position = jax.random.randint(random_keys[4], (GRID_AREAS, 2), 0, HORIZON_SECTIONS)
    section_numbers = jnp.arange(HORIZON_SECTIONS, dtype=jnp.int32)
    outage_struck = jnp.any(section_numbers[None, :, None] == outage_position[:, None, :], axis=-1).astype(jnp.float32)
    outage_deficit = jax.random.uniform(random_keys[5], (GRID_AREAS, HORIZON_SECTIONS, AREA_STATES), minval=0.22, maxval=0.6)
    decay_rate = decay_rate + outage_struck[:, :, None] * outage_deficit
    return jnp.exp(-decay_rate).astype(jnp.float32)


def draw_band_coef(key, part):
    first_key, second_key = jax.random.split(jax.random.fold_in(key, 7))
    shape = (GRID_AREAS, HORIZON_SECTIONS, NB, AREA_STATES)
    magnitude = jnp.exp(jax.random.uniform(first_key, shape, minval=math.log(0.05), maxval=math.log(0.1)))
    flip = jax.random.uniform(second_key, shape) < 0.5
    return jnp.where(flip, -magnitude, magnitude).astype(jnp.float32)


def draw_band_offsets(key, part):
    sign_values = jax.random.randint(key, (GRID_AREAS, NB - 2), 0, 2) * 2 - 1
    fixed_ends = jnp.broadcast_to(jnp.array([MAXOFF, -MAXOFF], jnp.int32), (GRID_AREAS, 2))
    return jnp.concatenate([fixed_ends, (MAXOFF * sign_values).astype(jnp.int32)], axis=1)


def draw_boundary_index(key, part):

    def draw_row(row_key):
        first_key, second_key = jax.random.split(row_key)
        middle = (jax.random.permutation(first_key, AREA_STATES - 2)[:NBD - 2] + 1).astype(jnp.int32)
        chosen = jnp.concatenate([jnp.array([0, AREA_STATES - 1], jnp.int32), middle])
        return chosen[jax.random.permutation(second_key, NBD)]
    return jax.vmap(draw_row)(jax.random.split(key, GRID_AREAS)).astype(jnp.int32)


def draw_adjacency(key, part):
    first_key, second_key = jax.random.split(key)
    own_ids = jnp.arange(GRID_AREAS, dtype=jnp.int32)[:, None]
    first_jump = jax.random.randint(first_key, (GRID_AREAS, 1), 1, GRID_AREAS)
    leading = (own_ids + first_jump) % GRID_AREAS
    others = jax.random.randint(second_key, (GRID_AREAS, NNB - 1), 0, GRID_AREAS)
    return jnp.concatenate([leading, others], axis=1).astype(jnp.int32)


def block_scale(key, dims, shards, smallest, high):
    factor_of, own = 1.0, jax.random.fold_in(key, 6)
    for position, blocks in shards:
        heights = jnp.exp(jax.random.uniform(jax.random.fold_in(own, position), (blocks,), jnp.float32, smallest / len(shards), high / len(shards)))
        factor_of = factor_of * jnp.repeat(heights, dims[position] // blocks).reshape([-1 if axis == position else 1 for axis in range(len(dims))])
    return factor_of


def bell_draw(key, shape, spread, limit, cuts=(), held_as=jnp.bfloat16):
    values = spread * jax.random.normal(key, shape, jnp.float32)
    if cuts:
        values = values * block_scale(key, shape, cuts, -0.22, 0.18)
    return jnp.clip(values, -limit, limit).astype(held_as)


def setup_inputs(seed: int = 0) -> dict:
    key_of = jax.random.split(jax.random.key(seed), 13)
    diagonal = draw_diagonal(jax.random.fold_in(key_of[12], 71), 0)
    band_coef = draw_band_coef(jax.random.fold_in(key_of[12], 71), 0)
    band_offsets = draw_band_offsets(jax.random.fold_in(key_of[12], 71), 0)
    boundary_index = draw_boundary_index(jax.random.fold_in(key_of[12], 71), 0)
    adjacency = draw_adjacency(jax.random.fold_in(key_of[12], 71), 0)
    start_state = bell_draw(key_of[5], (GRID_AREAS, AREA_STATES), 1.0, 6.0, ((0, 8),), jnp.float32)
    input_matrix = bell_draw(key_of[6], (GRID_AREAS, AREA_STATES, NU), AREA_STATES ** -0.5, 0.3125, ((0, 8),), jnp.float32)
    input_penalty = jnp.clip(jnp.exp(math.log(2.0) - 1.3862944 * jax.random.uniform(key_of[7], (GRID_AREAS, NU), jnp.float32) ** block_scale(key_of[7], (GRID_AREAS, NU), ((0, 8),), -0.2, 0.2)), 0.5, 2.0)
    linear_cost = bell_draw(key_of[8], (GRID_AREAS, HORIZON_SECTIONS, SCENS, AREA_STATES), 0.2, 1.2, ((0, 8), (1, 16), (2, 4)), jnp.float32)
    disturbance = bell_draw(key_of[9], (GRID_AREAS, HORIZON_SECTIONS, SCENS, AREA_STATES), 0.1, 0.6, ((0, 8), (1, 16), (2, 4)), jnp.float32)
    consensus = bell_draw(key_of[10], (GRID_AREAS, HORIZON_SECTIONS, SCENS, NBD), 0.3, 1.8, ((0, 8), (1, 16), (2, 4)), jnp.float32)
    dual_values = bell_draw(key_of[11], (GRID_AREAS, HORIZON_SECTIONS, SCENS, NBD), 0.3, 1.8, ((0, 8), (1, 16), (2, 4)), jnp.float32)
    return dict(diagonal=diagonal, band_coef=band_coef, band_offsets=band_offsets, boundary_index=boundary_index, adjacency=adjacency, start_state=start_state, input_matrix=input_matrix, input_penalty=input_penalty, linear_cost=linear_cost, disturbance=disturbance, consensus=consensus, dual_values=dual_values)


highest = lax.Precision.HIGHEST


def shifted(values, offset):
    extent = values.shape[-1]
    padding = [(0, 0)] * (values.ndim - 1) + [(MAXOFF, MAXOFF)]
    padded = jnp.pad(values, padding)
    return lax.dynamic_slice_in_dim(padded, (MAXOFF + offset).astype(jnp.int32), extent, values.ndim - 1)


def forward_apply(values, diag_row, band_rows, offsets):
    result = diag_row * values
    for band_index in range(band_rows.shape[0]):
        result = result + band_rows[band_index] * shifted(values, offsets[band_index])
    return result


def backward_apply(values, diag_row, band_rows, offsets):
    result = diag_row * values
    for band_index in range(band_rows.shape[0]):
        result = result + shifted(band_rows[band_index] * values, -offsets[band_index])
    return result


def area_pass(inputs):
    diagonals, band_rows, offsets, boundary_row, start_row, matrix, penalty, cost_rows, noise_rows, agreed_rows, dual_rows = inputs
    selection = (jnp.arange(AREA_STATES)[:, None] == boundary_row[None, :]).astype(jnp.float32)
    gradient = cost_rows + jnp.einsum("tsk,ik->tsi", dual_rows - agreed_rows, selection, precision=highest)

    def back_step(costate_next, section_inputs):
        diag_row, band_section, grad_row = section_inputs
        return backward_apply(costate_next, diag_row, band_section, offsets) + grad_row, costate_next

    zero_rows = jnp.zeros(cost_rows.shape[1:], jnp.float32)
    unused_first, costate_after = lax.scan(back_step, zero_rows, (diagonals, band_rows, gradient), reverse=True)
    controls = -jnp.einsum("tsi,iu->tsu", costate_after, matrix, precision=highest) / penalty
    shared = jnp.mean(controls[0], axis=0)
    controls = jnp.concatenate([jnp.broadcast_to(shared, controls[0].shape)[None], controls[1:]], axis=0)
    forcing = jnp.einsum("tsu,iu->tsi", controls, matrix, precision=highest) + noise_rows

    def ahead_step(state_now, section_inputs):
        diag_row, band_section, force_row = section_inputs
        return forward_apply(state_now, diag_row, band_section, offsets) + force_row, state_now

    initial = jnp.broadcast_to(start_row, zero_rows.shape)
    unused_last, trajectory = lax.scan(ahead_step, initial, (diagonals, band_rows, forcing))
    boundary = jnp.einsum("tsi,ik->tsk", trajectory, selection, precision=highest)
    return trajectory, boundary


def reference(diagonal, band_coef, band_offsets, boundary_index, adjacency, start_state, input_matrix, input_penalty, linear_cost, disturbance, consensus, dual_values):
    trajectory, boundary = lax.map(area_pass, (diagonal, band_coef, band_offsets, boundary_index, start_state, input_matrix, input_penalty, linear_cost, disturbance, consensus, dual_values))
    area_ids = jnp.arange(GRID_AREAS)
    weights = (area_ids[:, None] == area_ids[None, :]).astype(jnp.float32)
    weights = weights + jnp.sum((adjacency[:, :, None] == area_ids[None, None, :]).astype(jnp.float32), axis=1)
    agreed = jnp.einsum("an,ntsk->atsk", weights, boundary, precision=highest) / (NNB + 1)
    updated = dual_values + boundary - agreed
    return trajectory, agreed, updated
```

```python
import functools

import jax
import jax.numpy as jnp
from jax import lax
from jax.experimental import pallas as pl
from jax.experimental.pallas import tpu as pltpu
from jax.sharding import PartitionSpec as P

STEP = 16
NNB = 3

highest = lax.Precision.HIGHEST


def product(left, right):
    return jnp.dot(left, right, precision=highest, preferred_element_type=jnp.float32)


def product_transposed(left, right):
    return lax.dot_general(
        left, right, (((1,), (1,)), ((), ())), precision=highest, preferred_element_type=jnp.float32
    )


def kernel(
    segments,
    sharers,
    areas,
    offsets_ref,
    adjacency_ref,
    diagonal_ref,
    band_ref,
    index_ref,
    start_ref,
    matrix_ref,
    penalty_ref,
    cost_ref,
    noise_ref,
    consensus_ref,
    dual_ref,
    trajectory_ref,
    agreed_ref,
    updated_ref,
    grad_buf,
    pack_buf,
    pack_in,
    noise_buf,
    noise_in,
    part_buf,
    part_in,
    mean_buf,
    mean_in,
    costate_buf,
    force_buf,
    state_buf,
    state_in,
    boundary_buf,
    boundary_in,
    pack_send,
    pack_recv,
    noise_send,
    noise_recv,
    part_send,
    part_recv,
    mean_send,
    mean_recv,
    state_send,
    state_recv,
    boundary_send,
    boundary_recv,
):
    place = lax.axis_index("hor")
    share = lax.axis_index("scen")
    area = lax.axis_index("area")
    scens = segments
    extent = diagonal_ref.shape[-1]

    barrier = pltpu.get_barrier_semaphore()

    def greet(axis, own, count):
        def body(k, carry):
            pl.semaphore_signal(
                barrier,
                inc=1,
                device_id={axis: lax.rem(own + k, count)},
                device_id_type=pl.DeviceIdType.MESH,
            )
            return carry

        lax.fori_loop(1, count, body, 0)

    greet("hor", place, segments)
    greet("scen", share, sharers)
    greet("area", area, areas)

    selection = (
        lax.broadcasted_iota(jnp.int32, (extent, index_ref.shape[-1]), 0) == index_ref[...]
    ).astype(jnp.float32)
    for t in range(2):
        grad_buf[pl.ds(t * scens, scens), :] = cost_ref[0, t] + product_transposed(
            dual_ref[0, t] - consensus_ref[0, t], selection
        )
        part_buf[pl.ds(t, 1), :] = jnp.sum(
            grad_buf[pl.ds(t * scens, scens), :], axis=0, keepdims=True
        )
    lane = lax.broadcasted_iota(jnp.int32, (1, extent), 1)
    rows = []
    for t in range(2):
        up = jnp.zeros((1, extent), jnp.float32)
        down = jnp.zeros((1, extent), jnp.float32)
        for b in range(band_ref.shape[2]):
            coef = band_ref[0, t, pl.ds(b, 1), :]
            ahead = jnp.where(offsets_ref[0, b] > 0, 1.0, 0.0)
            up = up + ahead * coef
            down = down + (1.0 - ahead) * coef
        up = jnp.where(lane >= extent - STEP, 0.0, up)
        down = jnp.where(lane < STEP, 0.0, down)
        rows.append((diagonal_ref[0, pl.ds(t, 1), :], up, down))
    for s in range(scens):
        for t in range(2):
            pack_buf[s, pl.ds(t, 1), :] = grad_buf[pl.ds(t * scens + s, 1), :]
            noise_buf[s, pl.ds(t, 1), :] = noise_ref[0, t, pl.ds(s, 1), :]
            for c in range(3):
                pack_buf[s, pl.ds(2 + 3 * t + c, 1), :] = rows[t][c]
    pack_in[place] = pack_buf[place]
    noise_in[place] = noise_buf[place]
    part_in[share] = part_buf[...]

    pl.semaphore_wait(barrier, segments + sharers + areas - 3)

    def copy_to(axis, own, other, source, target, send, recv):
        return pltpu.make_async_remote_copy(
            src_ref=source,
            dst_ref=target.at[own],
            send_sem=send.at[other],
            recv_sem=recv.at[own],
            device_id={axis: other},
            device_id_type=pl.DeviceIdType.MESH,
        )

    def each(count, own, action):
        def body(k, carry):
            action(lax.rem(own + k, count))
            return carry

        lax.fori_loop(1, count, body, 0)

    def part_copy(other):
        return copy_to("scen", share, other, part_buf, part_in, part_send, part_recv)

    def pack_copy(other):
        return copy_to("hor", place, other, pack_buf.at[other], pack_in, pack_send, pack_recv)

    def noise_copy(other):
        return copy_to("hor", place, other, noise_buf.at[other], noise_in, noise_send, noise_recv)

    def mean_copy(other):
        return copy_to("hor", place, other, mean_buf, mean_in, mean_send, mean_recv)

    def state_copy(other):
        return copy_to("hor", place, other, state_buf.at[other], state_in, state_send, state_recv)

    def boundary_copy(other):
        return copy_to(
            "area", area, other, boundary_buf, boundary_in, boundary_send, boundary_recv
        )

    def arrived(axis, other, source, target, send, recv):
        pltpu.make_async_remote_copy(
            src_ref=source,
            dst_ref=target.at[other],
            send_sem=send.at[other],
            recv_sem=recv.at[other],
            device_id={axis: other},
            device_id_type=pl.DeviceIdType.MESH,
        ).wait_recv()

    each(sharers, share, lambda o: part_copy(o).start())
    each(segments, place, lambda o: pack_copy(o).start())
    each(
        sharers, share, lambda o: arrived("scen", o, part_buf, part_in, part_send, part_recv)
    )
    total = part_in[0]
    for k in range(1, sharers):
        total = total + part_in[k]
    mean_buf[...] = total * (1.0 / (scens * sharers))
    mean_in[place] = mean_buf[...]
    each(segments, place, lambda o: mean_copy(o).start())
    each(segments, place, lambda o: noise_copy(o).start())
    each(
        segments,
        place,
        lambda o: arrived("hor", o, pack_buf.at[o], pack_in, pack_send, pack_recv),
    )
    each(segments, place, lambda o: arrived("hor", o, mean_buf, mean_in, mean_send, mean_recv))

    first = lax.broadcasted_iota(jnp.int32, (8, extent), 0) == 0

    def wide(row):
        return jnp.broadcast_to(row, (8, extent))

    def back(k, costate):
        h = segments - 1 - k
        for j in (1, 0):
            costate_buf[pl.ds(2 * h + j, 1), :] = costate[0:1, :]
            diag, up, down = (
                wide(pack_in[h, pl.ds(2 + 3 * j + c, 1), :]) for c in range(3)
            )
            grad = jnp.where(
                first, wide(pack_in[h, pl.ds(j, 1), :]), wide(mean_in[h, pl.ds(j, 1), :])
            )
            if j == 0:
                costate_buf[pl.ds(2 * segments, 8), :] = costate
            costate = (
                (diag * costate + grad)
                + pltpu.roll(up * costate, STEP, 1)
                + pltpu.roll(down * costate, extent - STEP, 1)
            )
        return costate

    lax.fori_loop(0, segments, back, jnp.zeros((8, extent), jnp.float32))

    controls = -product(costate_buf[...], matrix_ref[0]) / penalty_ref[...]
    shared = controls[2 * segments + 1 : 2 * segments + 2, :]
    controls = controls[0 : 2 * segments, :]
    at_start = lax.broadcasted_iota(jnp.int32, controls.shape, 0) == 0
    controls = jnp.where(at_start, jnp.broadcast_to(shared, controls.shape), controls)
    force_buf[...] = product_transposed(controls, matrix_ref[0])
    each(
        segments,
        place,
        lambda o: arrived("hor", o, noise_buf.at[o], noise_in, noise_send, noise_recv),
    )

    def ahead_step(h, state):
        for j in (0, 1):
            state_buf[h, pl.ds(j, 1), :] = state[0:1, :]
            diag, up, down = (
                wide(pack_in[h, pl.ds(2 + 3 * j + c, 1), :]) for c in range(3)
            )
            force = wide(force_buf[pl.ds(2 * h + j, 1), :] + noise_in[h, pl.ds(j, 1), :])
            state = (
                (diag * state + force)
                + up * pltpu.roll(state, extent - STEP, 1)
                + down * pltpu.roll(state, STEP, 1)
            )

        @pl.when(h != place)
        def _():
            state_copy(h).start()

        return state

    lax.fori_loop(0, segments, ahead_step, wide(start_ref[...]))
    state_in[place] = state_buf[place]
    each(
        segments,
        place,
        lambda o: arrived("hor", o, state_buf.at[o], state_in, state_send, state_recv),
    )
    for s in range(scens):
        for t in range(2):
            trajectory_ref[0, t, pl.ds(s, 1), :] = state_in[s, pl.ds(t, 1), :]
    for t in range(2):
        boundary_buf[t] = product(trajectory_ref[0, t], selection)
    each(areas, area, lambda o: boundary_copy(o).start())
    boundary_in[area] = boundary_buf[...]
    each(
        areas,
        area,
        lambda o: arrived("area", o, boundary_buf, boundary_in, boundary_send, boundary_recv),
    )
    summed = boundary_buf[...]
    for n in range(areas):
        weight = jnp.float32(0.0)
        for j in range(NNB):
            weight = weight + jnp.where(adjacency_ref[0, j] == n, 1.0, 0.0)
        summed = summed + weight * boundary_in[n]
    agreed = summed * (1.0 / (NNB + 1))
    agreed_ref[0] = agreed
    updated_ref[0] = dual_ref[0] + boundary_buf[...] - agreed

    each(sharers, share, lambda o: part_copy(o).wait_send())

    def drain(o):
        pack_copy(o).wait_send()
        mean_copy(o).wait_send()
        noise_copy(o).wait_send()
        state_copy(o).wait_send()

    each(segments, place, drain)
    each(areas, area, lambda o: boundary_copy(o).wait_send())


def per_device(
    diagonal,
    band_coef,
    band_offsets,
    boundary_index,
    adjacency,
    start_state,
    input_matrix,
    input_penalty,
    linear_cost,
    disturbance,
    consensus,
    dual_values,
):
    segments = lax.axis_size("hor")
    sharers = lax.axis_size("scen")
    areas = lax.axis_size("area")
    extent = diagonal.shape[-1]
    vmem = pl.BlockSpec(memory_space=pltpu.VMEM)
    smem = pl.BlockSpec(memory_space=pltpu.SMEM)
    real = jnp.float32
    scratch = [
        pltpu.VMEM((2 * segments, extent), real),
        pltpu.VMEM((segments, 8, extent), real),
        pltpu.VMEM((segments, 8, extent), real),
        pltpu.VMEM((segments, 2, extent), real),
        pltpu.VMEM((segments, 2, extent), real),
        pltpu.VMEM((2, extent), real),
        pltpu.VMEM((sharers, 2, extent), real),
        pltpu.VMEM((2, extent), real),
        pltpu.VMEM((segments, 2, extent), real),
        pltpu.VMEM((2 * segments + 8, extent), real),
        pltpu.VMEM((2 * segments, extent), real),
        pltpu.VMEM((segments, 2, extent), real),
        pltpu.VMEM((segments, 2, extent), real),
        pltpu.VMEM(dual_values.shape[1:], real),
        pltpu.VMEM((areas, *dual_values.shape[1:]), real),
    ]
    for count in (segments, segments, sharers, segments, segments, areas):
        scratch += [pltpu.SemaphoreType.DMA((count,)), pltpu.SemaphoreType.DMA((count,))]
    return pl.pallas_call(
        functools.partial(kernel, segments, sharers, areas),
        out_shape=(
            jax.ShapeDtypeStruct(linear_cost.shape, real),
            jax.ShapeDtypeStruct(dual_values.shape, real),
            jax.ShapeDtypeStruct(dual_values.shape, real),
        ),
        in_specs=[smem] * 2 + [vmem] * 10,
        out_specs=(vmem,) * 3,
        scratch_shapes=scratch,
        compiler_params=pltpu.CompilerParams(collective_id=0, has_side_effects=True),
    )(
        band_offsets,
        adjacency,
        diagonal,
        band_coef,
        boundary_index,
        start_state,
        input_matrix,
        input_penalty,
        linear_cost,
        disturbance,
        consensus,
        dual_values,
    )


def solution(mesh):
    in_specs = (
        P("area", "hor", None),
        P("area", "hor", None, None),
        P("area", None),
        P("area", None),
        P("area", None),
        P("area", None),
        P("area", None, None),
        P("area", None),
        P("area", "hor", "scen", None),
        P("area", "hor", "scen", None),
        P("area", "hor", "scen", None),
        P("area", "hor", "scen", None),
    )
    out_specs = (
        P("area", "hor", "scen", None),
        P("area", "hor", "scen", None),
        P("area", "hor", "scen", None),
    )
    return jax.shard_map(
        per_device, mesh=mesh, in_specs=in_specs, out_specs=out_specs, check_vma=False
    )
```

```python
import functools

import jax
import jax.numpy as jnp
from jax import lax
from jax.experimental import pallas as pl
from jax.experimental.pallas import tpu as pltpu
from jax.sharding import PartitionSpec as P

STEP = 16
NNB = 3

highest = lax.Precision.HIGHEST


def product(left, right):
    return jnp.dot(left, right, precision=highest, preferred_element_type=jnp.float32)


def product_transposed(left, right):
    return lax.dot_general(
        left, right, (((1,), (1,)), ((), ())), precision=highest, preferred_element_type=jnp.float32
    )


def kernel(
    segments,
    sharers,
    areas,
    offsets_hbm,
    adjacency_hbm,
    diagonal_hbm,
    band_hbm,
    index_hbm,
    start_hbm,
    matrix_hbm,
    penalty_hbm,
    cost_hbm,
    noise_hbm,
    consensus_hbm,
    dual_hbm,
    trajectory_hbm,
    agreed_hbm,
    updated_hbm,
    offsets_ref,
    adjacency_ref,
    diagonal_ref,
    band_ref,
    index_ref,
    start_ref,
    matrix_ref,
    penalty_ref,
    cost_ref,
    noise_ref,
    consensus_ref,
    dual_ref,
    trajectory_ref,
    agreed_ref,
    updated_ref,
    grad_buf,
    coef_in,
    pack_buf,
    pack_in,
    noise_buf,
    noise_in,
    part_buf,
    part_in,
    mean_buf,
    mean_in,
    costate_buf,
    force_buf,
    state_buf,
    state_in,
    boundary_buf,
    boundary_in,
    fetch_sem,
    coef_send,
    pass_send,
    coef_recv,
    pack_send,
    pack_recv,
    noise_send,
    noise_recv,
    part_send,
    part_recv,
    mean_send,
    mean_recv,
    state_send,
    state_recv,
    boundary_send,
    boundary_recv,
):
    place = lax.axis_index("hor")
    share = lax.axis_index("scen")
    area = lax.axis_index("area")
    scens = segments
    extent = diagonal_ref.shape[-1]

    barrier = pltpu.get_barrier_semaphore()

    def greet(axis, own, count):
        def body(k, carry):
            pl.semaphore_signal(
                barrier,
                inc=1,
                device_id={axis: lax.rem(own + k, count)},
                device_id_type=pl.DeviceIdType.MESH,
            )
            return carry

        lax.fori_loop(1, count, body, 0)

    greet("hor", place, segments)
    greet("scen", share, sharers)
    greet("area", area, areas)

    fetches = [
        pltpu.make_async_copy(source, target, fetch_sem.at[k])
        for k, (source, target) in enumerate(
            (
                (offsets_hbm, offsets_ref),
                (band_hbm, band_ref),
                (diagonal_hbm, diagonal_ref),
                (index_hbm, index_ref),
                (dual_hbm, dual_ref),
                (consensus_hbm, consensus_ref),
                (cost_hbm, cost_ref),
                (noise_hbm, noise_ref),
                (matrix_hbm, matrix_ref),
                (penalty_hbm, penalty_ref),
                (start_hbm, start_ref),
                (adjacency_hbm, adjacency_ref),
            )
        )
    ]
    for fetch in fetches:
        fetch.start()
    for fetch in fetches[:8]:
        fetch.wait()

    selection = (
        lax.broadcasted_iota(jnp.int32, (extent, index_ref.shape[-1]), 0) == index_ref[...]
    ).astype(jnp.float32)
    for t in range(2):
        grad_buf[pl.ds(t * scens, scens), :] = cost_ref[0, t] + product_transposed(
            dual_ref[0, t] - consensus_ref[0, t], selection
        )
        part_buf[pl.ds(t, 1), :] = jnp.sum(
            grad_buf[pl.ds(t * scens, scens), :], axis=0, keepdims=True
        )
    lane = lax.broadcasted_iota(jnp.int32, (1, extent), 1)
    for t in range(2):
        up = jnp.zeros((1, extent), jnp.float32)
        down = jnp.zeros((1, extent), jnp.float32)
        for b in range(band_ref.shape[2]):
            coef = band_ref[0, t, pl.ds(b, 1), :]
            ahead = jnp.where(offsets_ref[0, b] > 0, 1.0, 0.0)
            up = up + ahead * coef
            down = down + (1.0 - ahead) * coef
        up = jnp.where(lane >= extent - STEP, 0.0, up)
        down = jnp.where(lane < STEP, 0.0, down)
        for c, row in enumerate((diagonal_ref[0, pl.ds(t, 1), :], up, down)):
            coef_in[place, c, pl.ds(t, 1), :] = row
    for s in range(scens):
        for t in range(2):
            pack_buf[s, pl.ds(t, 1), :] = grad_buf[pl.ds(t * scens + s, 1), :]
            noise_buf[s, pl.ds(t, 1), :] = noise_ref[0, t, pl.ds(s, 1), :]
    pack_in[place] = pack_buf[place]
    noise_in[place] = noise_buf[place]
    part_in[share] = part_buf[...]

    pl.semaphore_wait(barrier, segments + sharers + areas - 3)

    def copy_to(axis, own, other, source, target, send, recv):
        return pltpu.make_async_remote_copy(
            src_ref=source,
            dst_ref=target.at[own],
            send_sem=send.at[other],
            recv_sem=recv.at[own],
            device_id={axis: other},
            device_id_type=pl.DeviceIdType.MESH,
        )

    def each(count, own, action):
        def body(k, carry):
            action(lax.rem(own + k, count))
            return carry

        lax.fori_loop(1, count, body, 0)

    partner = place + 1 - 2 * lax.rem(place, 2)

    def coef_copy(slot, other, sem):
        return pltpu.make_async_remote_copy(
            src_ref=coef_in.at[slot],
            dst_ref=coef_in.at[slot],
            send_sem=sem,
            recv_sem=coef_recv.at[slot],
            device_id={"hor": other},
            device_id_type=pl.DeviceIdType.MESH,
        )

    def each_chip(action):
        def body(k, carry):
            action(lax.rem(place + 2 * k, segments))
            return carry

        lax.fori_loop(1, segments // 2, body, 0)

    def part_copy(other):
        return copy_to("scen", share, other, part_buf, part_in, part_send, part_recv)

    def pack_copy(other):
        return copy_to("hor", place, other, pack_buf.at[other], pack_in, pack_send, pack_recv)

    def noise_copy(other):
        return copy_to("hor", place, other, noise_buf.at[other], noise_in, noise_send, noise_recv)

    def mean_copy(other):
        return copy_to("hor", place, other, mean_buf, mean_in, mean_send, mean_recv)

    def state_copy(other):
        return copy_to("hor", place, other, state_buf.at[other], state_in, state_send, state_recv)

    def boundary_copy(other):
        return copy_to(
            "area", area, other, boundary_buf, boundary_in, boundary_send, boundary_recv
        )

    def arrived(axis, other, source, target, send, recv):
        pltpu.make_async_remote_copy(
            src_ref=source,
            dst_ref=target.at[other],
            send_sem=send.at[other],
            recv_sem=recv.at[other],
            device_id={axis: other},
            device_id_type=pl.DeviceIdType.MESH,
        ).wait_recv()

    each(sharers, share, lambda o: part_copy(o).start())
    each_chip(lambda o: coef_copy(place, o, coef_send.at[o]).start())
    coef_copy(place, partner, pass_send.at[place]).start()
    each(segments, place, lambda o: pack_copy(o).start())
    each(
        sharers, share, lambda o: arrived("scen", o, part_buf, part_in, part_send, part_recv)
    )
    total = part_in[0]
    for k in range(1, sharers):
        total = total + part_in[k]
    mean_buf[...] = total * (1.0 / (scens * sharers))
    mean_in[place] = mean_buf[...]
    each(segments, place, lambda o: mean_copy(o).start())
    each(segments, place, lambda o: noise_copy(o).start())

    def relay(o):
        coef_copy(o, o, coef_send.at[o]).wait_recv()
        coef_copy(o, partner, pass_send.at[o]).start()

    each_chip(relay)
    coef_copy(partner, partner, pass_send.at[partner]).wait_recv()
    each_chip(
        lambda o: coef_copy(
            o + partner - place, partner, pass_send.at[o + partner - place]
        ).wait_recv()
    )

    first = lax.broadcasted_iota(jnp.int32, (8, extent), 0) == 0

    def wide(row):
        return jnp.broadcast_to(row, (8, extent))

    def back(k, costate):
        h = segments - 1 - k

        @pl.when(h != place)
        def _():
            arrived("hor", h, pack_buf.at[h], pack_in, pack_send, pack_recv)
            arrived("hor", h, mean_buf, mean_in, mean_send, mean_recv)

        for j in (1, 0):
            costate_buf[pl.ds(2 * h + j, 1), :] = costate[0:1, :]
            diag, up, down = (
                wide(coef_in[h, c, pl.ds(j, 1), :]) for c in range(3)
            )
            grad = jnp.where(
                first, wide(pack_in[h, pl.ds(j, 1), :]), wide(mean_in[h, pl.ds(j, 1), :])
            )
            if j == 0:
                costate_buf[pl.ds(2 * segments, 8), :] = costate
            costate = (
                (diag * costate + grad)
                + pltpu.roll(up * costate, STEP, 1)
                + pltpu.roll(down * costate, extent - STEP, 1)
            )
        return costate

    lax.fori_loop(0, segments, back, jnp.zeros((8, extent), jnp.float32))

    for fetch in fetches[8:]:
        fetch.wait()
    controls = -product(costate_buf[...], matrix_ref[0]) / penalty_ref[...]
    shared = controls[2 * segments + 1 : 2 * segments + 2, :]
    controls = controls[0 : 2 * segments, :]
    at_start = lax.broadcasted_iota(jnp.int32, controls.shape, 0) == 0
    controls = jnp.where(at_start, jnp.broadcast_to(shared, controls.shape), controls)
    force_buf[...] = product_transposed(controls, matrix_ref[0])
    each(
        segments,
        place,
        lambda o: arrived("hor", o, noise_buf.at[o], noise_in, noise_send, noise_recv),
    )

    def ahead_step(h, state):
        for j in (0, 1):
            state_buf[h, pl.ds(j, 1), :] = state[0:1, :]
            diag, up, down = (
                wide(coef_in[h, c, pl.ds(j, 1), :]) for c in range(3)
            )
            force = wide(force_buf[pl.ds(2 * h + j, 1), :] + noise_in[h, pl.ds(j, 1), :])
            state = (
                (diag * state + force)
                + up * pltpu.roll(state, extent - STEP, 1)
                + down * pltpu.roll(state, STEP, 1)
            )

        @pl.when(h != place)
        def _():
            state_copy(h).start()

        return state

    lax.fori_loop(0, segments, ahead_step, wide(start_ref[...]))
    state_in[place] = state_buf[place]
    each(
        segments,
        place,
        lambda o: arrived("hor", o, state_buf.at[o], state_in, state_send, state_recv),
    )
    for s in range(scens):
        for t in range(2):
            trajectory_ref[0, t, pl.ds(s, 1), :] = state_in[s, pl.ds(t, 1), :]
    put_state = pltpu.make_async_copy(trajectory_ref, trajectory_hbm, fetch_sem.at[0])
    put_state.start()
    for t in range(2):
        boundary_buf[t] = product(trajectory_ref[0, t], selection)
    each(areas, area, lambda o: boundary_copy(o).start())
    boundary_in[area] = boundary_buf[...]
    each(
        areas,
        area,
        lambda o: arrived("area", o, boundary_buf, boundary_in, boundary_send, boundary_recv),
    )
    summed = boundary_buf[...]
    for n in range(areas):
        weight = jnp.float32(0.0)
        for j in range(NNB):
            weight = weight + jnp.where(adjacency_ref[0, j] == n, 1.0, 0.0)
        summed = summed + weight * boundary_in[n]
    agreed = summed * (1.0 / (NNB + 1))
    agreed_ref[0] = agreed
    updated_ref[0] = dual_ref[0] + boundary_buf[...] - agreed
    put_agreed = pltpu.make_async_copy(agreed_ref, agreed_hbm, fetch_sem.at[1])
    put_updated = pltpu.make_async_copy(updated_ref, updated_hbm, fetch_sem.at[2])
    put_agreed.start()
    put_updated.start()

    each(sharers, share, lambda o: part_copy(o).wait_send())

    def drain_chip(o):
        coef_copy(place, o, coef_send.at[o]).wait_send()
        coef_copy(o, partner, pass_send.at[o]).wait_send()

    each_chip(drain_chip)
    coef_copy(place, partner, pass_send.at[place]).wait_send()

    def drain(o):
        pack_copy(o).wait_send()
        mean_copy(o).wait_send()
        noise_copy(o).wait_send()
        state_copy(o).wait_send()

    each(segments, place, drain)
    each(areas, area, lambda o: boundary_copy(o).wait_send())
    put_state.wait()
    put_agreed.wait()
    put_updated.wait()


def per_device(
    diagonal,
    band_coef,
    band_offsets,
    boundary_index,
    adjacency,
    start_state,
    input_matrix,
    input_penalty,
    linear_cost,
    disturbance,
    consensus,
    dual_values,
):
    segments = lax.axis_size("hor")
    sharers = lax.axis_size("scen")
    areas = lax.axis_size("area")
    extent = diagonal.shape[-1]
    anywhere = pl.BlockSpec(memory_space=pl.ANY)
    real = jnp.float32
    scratch = [
        pltpu.SMEM(band_offsets.shape, jnp.int32),
        pltpu.SMEM(adjacency.shape, jnp.int32),
    ]
    scratch += [
        pltpu.VMEM(held.shape, held.dtype)
        for held in (
            diagonal,
            band_coef,
            boundary_index,
            start_state,
            input_matrix,
            input_penalty,
            linear_cost,
            disturbance,
            consensus,
            dual_values,
            linear_cost,
            dual_values,
            dual_values,
        )
    ]
    scratch += [
        pltpu.VMEM((2 * segments, extent), real),
        pltpu.VMEM((segments, 3, 2, extent), real),
        pltpu.VMEM((segments, 2, extent), real),
        pltpu.VMEM((segments, 2, extent), real),
        pltpu.VMEM((segments, 2, extent), real),
        pltpu.VMEM((segments, 2, extent), real),
        pltpu.VMEM((2, extent), real),
        pltpu.VMEM((sharers, 2, extent), real),
        pltpu.VMEM((2, extent), real),
        pltpu.VMEM((segments, 2, extent), real),
        pltpu.VMEM((2 * segments + 8, extent), real),
        pltpu.VMEM((2 * segments, extent), real),
        pltpu.VMEM((segments, 2, extent), real),
        pltpu.VMEM((segments, 2, extent), real),
        pltpu.VMEM(dual_values.shape[1:], real),
        pltpu.VMEM((areas, *dual_values.shape[1:]), real),
    ]
    scratch += [pltpu.SemaphoreType.DMA((12,))]
    scratch += [pltpu.SemaphoreType.DMA((segments,)) for _ in range(3)]
    for count in (segments, segments, sharers, segments, segments, areas):
        scratch += [pltpu.SemaphoreType.DMA((count,)), pltpu.SemaphoreType.DMA((count,))]
    return pl.pallas_call(
        functools.partial(kernel, segments, sharers, areas),
        out_shape=(
            jax.ShapeDtypeStruct(linear_cost.shape, real),
            jax.ShapeDtypeStruct(dual_values.shape, real),
            jax.ShapeDtypeStruct(dual_values.shape, real),
        ),
        in_specs=[anywhere] * 12,
        out_specs=(anywhere,) * 3,
        scratch_shapes=scratch,
        compiler_params=pltpu.CompilerParams(collective_id=0, has_side_effects=True),
    )(
        band_offsets,
        adjacency,
        diagonal,
        band_coef,
        boundary_index,
        start_state,
        input_matrix,
        input_penalty,
        linear_cost,
        disturbance,
        consensus,
        dual_values,
    )


def solution(mesh):
    in_specs = (
        P("area", "hor", None),
        P("area", "hor", None, None),
        P("area", None),
        P("area", None),
        P("area", None),
        P("area", None),
        P("area", None, None),
        P("area", None),
        P("area", "hor", "scen", None),
        P("area", "hor", "scen", None),
        P("area", "hor", "scen", None),
        P("area", "hor", "scen", None),
    )
    out_specs = (
        P("area", "hor", "scen", None),
        P("area", "hor", "scen", None),
        P("area", "hor", "scen", None),
    )
    return jax.shard_map(
        per_device, mesh=mesh, in_specs=in_specs, out_specs=out_specs, check_vma=False
    )
```

```python
import functools

import jax
import jax.numpy as jnp
from jax import lax
from jax.experimental import pallas as pl
from jax.experimental.pallas import tpu as pltpu
from jax.sharding import PartitionSpec as P

STEP = 16
NNB = 3
CHUNKS = 4

highest = lax.Precision.HIGHEST


def product(left, right):
    return jnp.dot(left, right, precision=highest, preferred_element_type=jnp.float32)


def product_transposed(left, right):
    return lax.dot_general(
        left, right, (((1,), (1,)), ((), ())), precision=highest, preferred_element_type=jnp.float32
    )


def picked(rows, selection):
    high = rows.astype(jnp.bfloat16).astype(jnp.float32)
    middle = (rows - high).astype(jnp.bfloat16).astype(jnp.float32)
    low = (rows - high) - middle
    count = rows.shape[0]
    parts = jnp.concatenate([high, middle, low, jnp.zeros_like(low)], axis=0)
    out = jnp.dot(parts.astype(jnp.bfloat16), selection, preferred_element_type=jnp.float32)
    return (out[0:count] + out[count : 2 * count]) + out[2 * count : 3 * count]


def kernel(
    segments,
    sharers,
    areas,
    offsets_hbm,
    adjacency_hbm,
    diagonal_hbm,
    band_hbm,
    index_hbm,
    start_hbm,
    matrix_hbm,
    penalty_hbm,
    cost_hbm,
    noise_hbm,
    consensus_hbm,
    dual_hbm,
    trajectory_hbm,
    agreed_hbm,
    updated_hbm,
    offsets_ref,
    adjacency_ref,
    diagonal_ref,
    band_ref,
    index_ref,
    start_ref,
    matrix_ref,
    penalty_ref,
    cost_ref,
    noise_ref,
    consensus_ref,
    dual_ref,
    trajectory_ref,
    agreed_ref,
    updated_ref,
    grad_buf,
    coef_in,
    pack_buf,
    pack_in,
    noise_buf,
    noise_in,
    part_buf,
    part_in,
    mean_buf,
    mean_in,
    costate_buf,
    force_buf,
    state_buf,
    state_in,
    boundary_buf,
    boundary_in,
    agreed_buf,
    agreed_in,
    fetch_sem,
    coef_send,
    pass_send,
    coef_recv,
    pack_send,
    pack_recv,
    noise_send,
    noise_recv,
    part_send,
    part_recv,
    mean_send,
    mean_recv,
    state_send,
    state_recv,
    boundary_send,
    boundary_recv,
    agreed_send,
    agreed_recv,
):
    place = lax.axis_index("hor")
    share = lax.axis_index("scen")
    area = lax.axis_index("area")
    scens = segments
    extent = diagonal_ref.shape[-1]

    barrier = pltpu.get_barrier_semaphore()

    def greet(axis, own, count):
        def body(k, carry):
            pl.semaphore_signal(
                barrier,
                inc=1,
                device_id={axis: lax.rem(own + k, count)},
                device_id_type=pl.DeviceIdType.MESH,
            )
            return carry

        lax.fori_loop(1, count, body, 0)

    greet("hor", place, segments)
    greet("scen", share, sharers)
    greet("area", area, areas)

    fetches = [
        pltpu.make_async_copy(source, target, fetch_sem.at[k])
        for k, (source, target) in enumerate(
            (
                (offsets_hbm, offsets_ref),
                (band_hbm, band_ref),
                (diagonal_hbm, diagonal_ref),
                (index_hbm, index_ref),
                (dual_hbm, dual_ref),
                (consensus_hbm, consensus_ref),
                (cost_hbm, cost_ref),
                (noise_hbm, noise_ref),
                (matrix_hbm, matrix_ref),
                (penalty_hbm, penalty_ref),
                (start_hbm, start_ref),
                (adjacency_hbm, adjacency_ref),
            )
        )
    ]
    for fetch in fetches:
        fetch.start()
    for fetch in fetches[:8]:
        fetch.wait()

    selection = (
        lax.broadcasted_iota(jnp.int32, (extent, index_ref.shape[-1]), 0) == index_ref[...]
    ).astype(jnp.float32)
    for t in range(2):
        grad_buf[pl.ds(t * scens, scens), :] = cost_ref[0, t] + product_transposed(
            dual_ref[0, t] - consensus_ref[0, t], selection
        )
        part_buf[pl.ds(t, 1), :] = jnp.sum(
            grad_buf[pl.ds(t * scens, scens), :], axis=0, keepdims=True
        )
    lane = lax.broadcasted_iota(jnp.int32, (1, extent), 1)
    for t in range(2):
        up = jnp.zeros((1, extent), jnp.float32)
        down = jnp.zeros((1, extent), jnp.float32)
        for b in range(band_ref.shape[2]):
            coef = band_ref[0, t, pl.ds(b, 1), :]
            ahead = jnp.where(offsets_ref[0, b] > 0, 1.0, 0.0)
            up = up + ahead * coef
            down = down + (1.0 - ahead) * coef
        up = jnp.where(lane >= extent - STEP, 0.0, up)
        down = jnp.where(lane < STEP, 0.0, down)
        for c, row in enumerate((diagonal_ref[0, pl.ds(t, 1), :], up, down)):
            coef_in[place, c, pl.ds(t, 1), :] = row
    for s in range(scens):
        for t in range(2):
            pack_buf[s, pl.ds(t, 1), :] = grad_buf[pl.ds(t * scens + s, 1), :]
            noise_buf[s, pl.ds(t, 1), :] = noise_ref[0, t, pl.ds(s, 1), :]
    pack_in[place] = pack_buf[place]
    noise_in[place] = noise_buf[place]
    part_in[share] = part_buf[...]

    pl.semaphore_wait(barrier, segments + sharers + areas - 3)

    def copy_to(axis, own, other, source, target, send, recv):
        return pltpu.make_async_remote_copy(
            src_ref=source,
            dst_ref=target.at[own],
            send_sem=send.at[other],
            recv_sem=recv.at[own],
            device_id={axis: other},
            device_id_type=pl.DeviceIdType.MESH,
        )

    def each(count, own, action):
        def body(k, carry):
            action(lax.rem(own + k, count))
            return carry

        lax.fori_loop(1, count, body, 0)

    partner = place + 1 - 2 * lax.rem(place, 2)

    def coef_copy(slot, other, sem):
        return pltpu.make_async_remote_copy(
            src_ref=coef_in.at[slot],
            dst_ref=coef_in.at[slot],
            send_sem=sem,
            recv_sem=coef_recv.at[slot],
            device_id={"hor": other},
            device_id_type=pl.DeviceIdType.MESH,
        )

    def each_chip(action):
        def body(k, carry):
            action(lax.rem(place + 2 * k, segments))
            return carry

        lax.fori_loop(1, segments // 2, body, 0)

    def part_copy(other):
        return copy_to("scen", share, other, part_buf, part_in, part_send, part_recv)

    def pack_copy(other):
        return copy_to("hor", place, other, pack_buf.at[other], pack_in, pack_send, pack_recv)

    def noise_copy(other):
        return copy_to("hor", place, other, noise_buf.at[other], noise_in, noise_send, noise_recv)

    def mean_copy(other):
        return copy_to("hor", place, other, mean_buf, mean_in, mean_send, mean_recv)

    def state_copy(other):
        return copy_to("hor", place, other, state_buf.at[other], state_in, state_send, state_recv)

    def boundary_copy(chunk, other):
        return pltpu.make_async_remote_copy(
            src_ref=boundary_buf.at[chunk],
            dst_ref=boundary_in.at[chunk, area],
            send_sem=boundary_send.at[chunk, other],
            recv_sem=boundary_recv.at[chunk, area],
            device_id={"area": other},
            device_id_type=pl.DeviceIdType.MESH,
        )

    def boundary_arrived(chunk, other):
        pltpu.make_async_remote_copy(
            src_ref=boundary_buf.at[chunk],
            dst_ref=boundary_in.at[chunk, other],
            send_sem=boundary_send.at[chunk, other],
            recv_sem=boundary_recv.at[chunk, other],
            device_id={"area": other},
            device_id_type=pl.DeviceIdType.MESH,
        ).wait_recv()

    def agreed_copy(other):
        return copy_to(
            "hor", place, other, agreed_buf.at[other], agreed_in, agreed_send, agreed_recv
        )

    def arrived(axis, other, source, target, send, recv):
        pltpu.make_async_remote_copy(
            src_ref=source,
            dst_ref=target.at[other],
            send_sem=send.at[other],
            recv_sem=recv.at[other],
            device_id={axis: other},
            device_id_type=pl.DeviceIdType.MESH,
        ).wait_recv()

    each(sharers, share, lambda o: part_copy(o).start())
    each_chip(lambda o: coef_copy(place, o, coef_send.at[o]).start())
    coef_copy(place, partner, pass_send.at[place]).start()
    each(segments, place, lambda o: pack_copy(o).start())
    each(
        sharers, share, lambda o: arrived("scen", o, part_buf, part_in, part_send, part_recv)
    )
    total = part_in[0]
    for k in range(1, sharers):
        total = total + part_in[k]
    mean_buf[...] = total * (1.0 / (scens * sharers))
    mean_in[place] = mean_buf[...]
    each(segments, place, lambda o: mean_copy(o).start())
    each(segments, place, lambda o: noise_copy(o).start())

    def relay(o):
        coef_copy(o, o, coef_send.at[o]).wait_recv()
        coef_copy(o, partner, pass_send.at[o]).start()

    each_chip(relay)
    coef_copy(partner, partner, pass_send.at[partner]).wait_recv()
    each_chip(
        lambda o: coef_copy(
            o + partner - place, partner, pass_send.at[o + partner - place]
        ).wait_recv()
    )

    first = lax.broadcasted_iota(jnp.int32, (8, extent), 0) == 0

    def wide(row):
        return jnp.broadcast_to(row, (8, extent))

    def back(k, costate):
        h = segments - 1 - k

        @pl.when(h != place)
        def _():
            arrived("hor", h, pack_buf.at[h], pack_in, pack_send, pack_recv)
            arrived("hor", h, mean_buf, mean_in, mean_send, mean_recv)

        for j in (1, 0):
            costate_buf[pl.ds(2 * h + j, 1), :] = costate[0:1, :]
            diag, up, down = (
                wide(coef_in[h, c, pl.ds(j, 1), :]) for c in range(3)
            )
            grad = jnp.where(
                first, wide(pack_in[h, pl.ds(j, 1), :]), wide(mean_in[h, pl.ds(j, 1), :])
            )
            if j == 0:
                costate_buf[pl.ds(2 * segments, 8), :] = costate
            costate = (
                (diag * costate + grad)
                + pltpu.roll(up * costate, STEP, 1)
                + pltpu.roll(down * costate, extent - STEP, 1)
            )
        return costate

    lax.fori_loop(0, segments, back, jnp.zeros((8, extent), jnp.float32))

    for fetch in fetches[8:]:
        fetch.wait()
    controls = -product(costate_buf[...], matrix_ref[0]) / penalty_ref[...]
    shared = controls[2 * segments + 1 : 2 * segments + 2, :]
    controls = controls[0 : 2 * segments, :]
    at_start = lax.broadcasted_iota(jnp.int32, controls.shape, 0) == 0
    controls = jnp.where(at_start, jnp.broadcast_to(shared, controls.shape), controls)
    force_buf[...] = product_transposed(controls, matrix_ref[0])
    each(
        segments,
        place,
        lambda o: arrived("hor", o, noise_buf.at[o], noise_in, noise_send, noise_recv),
    )

    def ahead_step(h, state):
        for j in (0, 1):
            state_buf[h, pl.ds(j, 1), :] = state[0:1, :]
            costate_buf[pl.ds(2 * h + j, 1), :] = state[0:1, :]
            diag, up, down = (
                wide(coef_in[h, c, pl.ds(j, 1), :]) for c in range(3)
            )
            force = wide(force_buf[pl.ds(2 * h + j, 1), :] + noise_in[h, pl.ds(j, 1), :])
            state = (
                (diag * state + force)
                + up * pltpu.roll(state, extent - STEP, 1)
                + down * pltpu.roll(state, STEP, 1)
            )

        @pl.when(h != place)
        def _():
            state_copy(h).start()

        return state

    narrow = selection.astype(jnp.bfloat16)
    chunks = boundary_buf.shape[0]
    span = segments // chunks
    state = wide(start_ref[...])
    for chunk in range(chunks):
        state = lax.fori_loop(chunk * span, (chunk + 1) * span, ahead_step, state)
        boundary_buf[chunk] = picked(
            costate_buf[pl.ds(2 * span * chunk, 2 * span), :], narrow
        )
        each(areas, area, lambda o, chunk=chunk: boundary_copy(chunk, o).start())
    state_in[place] = state_buf[place]

    weights = []
    for n in range(areas):
        weight = jnp.where(area == n, 1.0, 0.0)
        for j in range(NNB):
            weight = weight + jnp.where(adjacency_ref[0, j] == n, 1.0, 0.0)
        weights.append(weight * (1.0 / (NNB + 1)))
    for chunk in range(chunks):
        boundary_in[chunk, area] = boundary_buf[chunk]
        each(areas, area, lambda o, chunk=chunk: boundary_arrived(chunk, o))
        agreed = weights[0] * boundary_in[chunk, 0]
        for n in range(1, areas):
            agreed = agreed + weights[n] * boundary_in[chunk, n]
        for i in range(span):
            h = chunk * span + i
            agreed_buf[h] = agreed[2 * i : 2 * i + 2, :]

            @pl.when(h != place)
            def _(h=h):
                agreed_copy(h).start()

    agreed_in[place] = agreed_buf[place]
    each(
        segments,
        place,
        lambda o: arrived("hor", o, state_buf.at[o], state_in, state_send, state_recv),
    )
    for s in range(scens):
        for t in range(2):
            trajectory_ref[0, t, pl.ds(s, 1), :] = state_in[s, pl.ds(t, 1), :]
    put_state = pltpu.make_async_copy(trajectory_ref, trajectory_hbm, fetch_sem.at[0])
    put_state.start()
    own = [dual_ref[0, t] + picked(trajectory_ref[0, t], narrow) for t in range(2)]
    each(
        segments,
        place,
        lambda o: arrived("hor", o, agreed_buf.at[o], agreed_in, agreed_send, agreed_recv),
    )
    for s in range(scens):
        for t in range(2):
            agreed_ref[0, t, pl.ds(s, 1), :] = agreed_in[s, pl.ds(t, 1), :]
    for t in range(2):
        updated_ref[0, t] = own[t] - agreed_ref[0, t]
    put_agreed = pltpu.make_async_copy(agreed_ref, agreed_hbm, fetch_sem.at[1])
    put_updated = pltpu.make_async_copy(updated_ref, updated_hbm, fetch_sem.at[2])
    put_agreed.start()
    put_updated.start()

    each(sharers, share, lambda o: part_copy(o).wait_send())

    def drain_chip(o):
        coef_copy(place, o, coef_send.at[o]).wait_send()
        coef_copy(o, partner, pass_send.at[o]).wait_send()

    each_chip(drain_chip)
    coef_copy(place, partner, pass_send.at[place]).wait_send()

    def drain(o):
        pack_copy(o).wait_send()
        mean_copy(o).wait_send()
        noise_copy(o).wait_send()
        state_copy(o).wait_send()
        agreed_copy(o).wait_send()

    each(segments, place, drain)
    for chunk in range(chunks):
        each(areas, area, lambda o, chunk=chunk: boundary_copy(chunk, o).wait_send())
    put_state.wait()
    put_agreed.wait()
    put_updated.wait()


def per_device(
    diagonal,
    band_coef,
    band_offsets,
    boundary_index,
    adjacency,
    start_state,
    input_matrix,
    input_penalty,
    linear_cost,
    disturbance,
    consensus,
    dual_values,
):
    segments = lax.axis_size("hor")
    sharers = lax.axis_size("scen")
    areas = lax.axis_size("area")
    extent = diagonal.shape[-1]
    shared_count = dual_values.shape[-1]
    anywhere = pl.BlockSpec(memory_space=pl.ANY)
    real = jnp.float32
    scratch = [
        pltpu.SMEM(band_offsets.shape, jnp.int32),
        pltpu.SMEM(adjacency.shape, jnp.int32),
    ]
    scratch += [
        pltpu.VMEM(held.shape, held.dtype)
        for held in (
            diagonal,
            band_coef,
            boundary_index,
            start_state,
            input_matrix,
            input_penalty,
            linear_cost,
            disturbance,
            consensus,
            dual_values,
            linear_cost,
            dual_values,
            dual_values,
        )
    ]
    scratch += [
        pltpu.VMEM((2 * segments, extent), real),
        pltpu.VMEM((segments, 3, 2, extent), real),
        pltpu.VMEM((segments, 2, extent), real),
        pltpu.VMEM((segments, 2, extent), real),
        pltpu.VMEM((segments, 2, extent), real),
        pltpu.VMEM((segments, 2, extent), real),
        pltpu.VMEM((2, extent), real),
        pltpu.VMEM((sharers, 2, extent), real),
        pltpu.VMEM((2, extent), real),
        pltpu.VMEM((segments, 2, extent), real),
        pltpu.VMEM((2 * segments + 8, extent), real),
        pltpu.VMEM((2 * segments, extent), real),
        pltpu.VMEM((segments, 2, extent), real),
        pltpu.VMEM((segments, 2, extent), real),
        pltpu.VMEM((CHUNKS, 2 * segments // CHUNKS, shared_count), real),
        pltpu.VMEM((CHUNKS, areas, 2 * segments // CHUNKS, shared_count), real),
        pltpu.VMEM((segments, 2, shared_count), real),
        pltpu.VMEM((segments, 2, shared_count), real),
    ]
    scratch += [pltpu.SemaphoreType.DMA((12,))]
    scratch += [pltpu.SemaphoreType.DMA((segments,)) for _ in range(3)]
    for count in (segments, segments, sharers, segments, segments):
        scratch += [pltpu.SemaphoreType.DMA((count,)), pltpu.SemaphoreType.DMA((count,))]
    scratch += [pltpu.SemaphoreType.DMA((CHUNKS, areas)) for _ in range(2)]
    scratch += [pltpu.SemaphoreType.DMA((segments,)) for _ in range(2)]
    return pl.pallas_call(
        functools.partial(kernel, segments, sharers, areas),
        out_shape=(
            jax.ShapeDtypeStruct(linear_cost.shape, real),
            jax.ShapeDtypeStruct(dual_values.shape, real),
            jax.ShapeDtypeStruct(dual_values.shape, real),
        ),
        in_specs=[anywhere] * 12,
        out_specs=(anywhere,) * 3,
        scratch_shapes=scratch,
        compiler_params=pltpu.CompilerParams(collective_id=0, has_side_effects=True),
    )(
        band_offsets,
        adjacency,
        diagonal,
        band_coef,
        boundary_index,
        start_state,
        input_matrix,
        input_penalty,
        linear_cost,
        disturbance,
        consensus,
        dual_values,
    )


def solution(mesh):
    in_specs = (
        P("area", "hor", None),
        P("area", "hor", None, None),
        P("area", None),
        P("area", None),
        P("area", None),
        P("area", None),
        P("area", None, None),
        P("area", None),
        P("area", "hor", "scen", None),
        P("area", "hor", "scen", None),
        P("area", "hor", "scen", None),
        P("area", "hor", "scen", None),
    )
    out_specs = (
        P("area", "hor", "scen", None),
        P("area", "hor", "scen", None),
        P("area", "hor", "scen", None),
    )
    return jax.shard_map(
        per_device, mesh=mesh, in_specs=in_specs, out_specs=out_specs, check_vma=False
    )
```

```python
import functools

import jax
import jax.numpy as jnp
from jax import lax
from jax.experimental import pallas as pl
from jax.experimental.pallas import tpu as pltpu
from jax.sharding import PartitionSpec as P

STEP = 16
NNB = 3

highest = lax.Precision.HIGHEST


def product(left, right):
    return jnp.dot(left, right, precision=highest, preferred_element_type=jnp.float32)


def product_transposed(left, right):
    return lax.dot_general(
        left, right, (((1,), (1,)), ((), ())), precision=highest, preferred_element_type=jnp.float32
    )


def in_parts(rows):
    high = rows.astype(jnp.bfloat16).astype(jnp.float32)
    middle = (rows - high).astype(jnp.bfloat16).astype(jnp.float32)
    return high, middle, (rows - high) - middle


def picked(rows, selection):
    count = rows.shape[0]
    parts = list(in_parts(rows))
    if 3 * count % 16:
        parts.append(jnp.zeros((16 - 3 * count % 16, rows.shape[1]), jnp.float32))
    parts = jnp.concatenate(parts, axis=0).astype(jnp.bfloat16)
    out = jnp.dot(parts, selection, preferred_element_type=jnp.float32)
    return (out[0:count] + out[count : 2 * count]) + out[2 * count : 3 * count]


def finish(
    adjacency_ref, dual_ref, state_ref, boundary_ref, trajectory_ref, agreed_ref, updated_ref
):
    area = lax.axis_index("area")
    own = boundary_ref[area]
    summed = own
    for n in range(boundary_ref.shape[0]):
        weight = jnp.float32(0.0)
        for j in range(NNB):
            weight = weight + jnp.where(adjacency_ref[0, j] == n, 1.0, 0.0)
        summed = summed + weight * boundary_ref[n]
    agreed = summed * (1.0 / (NNB + 1))
    trajectory_ref[...] = state_ref[...]
    agreed_ref[0] = agreed
    updated_ref[0] = dual_ref[0] + own - agreed


def kernel(
    segments,
    sharers,
    areas,
    offsets_hbm,
    diagonal_hbm,
    band_hbm,
    index_hbm,
    start_hbm,
    matrix_hbm,
    penalty_hbm,
    cost_hbm,
    noise_hbm,
    consensus_hbm,
    dual_hbm,
    trajectory_hbm,
    boundary_in,
    offsets_ref,
    diagonal_ref,
    band_ref,
    index_ref,
    start_ref,
    matrix_ref,
    penalty_ref,
    cost_ref,
    noise_ref,
    consensus_ref,
    dual_ref,
    trajectory_ref,
    grad_buf,
    coef_in,
    pack_buf,
    pack_in,
    noise_buf,
    noise_in,
    part_buf,
    part_in,
    mean_buf,
    mean_in,
    costate_buf,
    force_buf,
    state_buf,
    state_in,
    boundary_buf,
    matrix_buf,
    fetch_sem,
    coef_send,
    pass_send,
    coef_recv,
    pack_send,
    pack_recv,
    noise_send,
    noise_recv,
    part_send,
    part_recv,
    mean_send,
    mean_recv,
    state_send,
    state_recv,
    boundary_send,
    boundary_recv,
):
    place = lax.axis_index("hor")
    share = lax.axis_index("scen")
    area = lax.axis_index("area")
    scens = segments
    extent = diagonal_ref.shape[-1]

    barrier = pltpu.get_barrier_semaphore()

    def greet(axis, own, count):
        def body(k, carry):
            pl.semaphore_signal(
                barrier,
                inc=1,
                device_id={axis: lax.rem(own + k, count)},
                device_id_type=pl.DeviceIdType.MESH,
            )
            return carry

        lax.fori_loop(1, count, body, 0)

    greet("hor", place, segments)
    greet("scen", share, sharers)
    greet("area", area, areas)

    fetches = [
        pltpu.make_async_copy(source, target, fetch_sem.at[k])
        for k, (source, target) in enumerate(
            (
                (offsets_hbm, offsets_ref),
                (band_hbm, band_ref),
                (diagonal_hbm, diagonal_ref),
                (index_hbm, index_ref),
                (dual_hbm, dual_ref),
                (consensus_hbm, consensus_ref),
                (cost_hbm, cost_ref),
                (noise_hbm, noise_ref),
                (matrix_hbm, matrix_ref),
                (penalty_hbm, penalty_ref),
                (start_hbm, start_ref),
            )
        )
    ]
    for fetch in fetches:
        fetch.start()
    for fetch in fetches[:8]:
        fetch.wait()

    selection = (
        lax.broadcasted_iota(jnp.int32, (extent, index_ref.shape[-1]), 0) == index_ref[...]
    ).astype(jnp.float32)
    for t in range(2):
        grad_buf[pl.ds(t * scens, scens), :] = cost_ref[0, t] + product_transposed(
            dual_ref[0, t] - consensus_ref[0, t], selection
        )
        part_buf[pl.ds(t, 1), :] = jnp.sum(
            grad_buf[pl.ds(t * scens, scens), :], axis=0, keepdims=True
        )
    lane = lax.broadcasted_iota(jnp.int32, (1, extent), 1)
    for t in range(2):
        up = jnp.zeros((1, extent), jnp.float32)
        down = jnp.zeros((1, extent), jnp.float32)
        for b in range(band_ref.shape[2]):
            coef = band_ref[0, t, pl.ds(b, 1), :]
            ahead = jnp.where(offsets_ref[0, b] > 0, 1.0, 0.0)
            up = up + ahead * coef
            down = down + (1.0 - ahead) * coef
        up = jnp.where(lane >= extent - STEP, 0.0, up)
        down = jnp.where(lane < STEP, 0.0, down)
        for c, row in enumerate((diagonal_ref[0, pl.ds(t, 1), :], up, down)):
            coef_in[place, c, pl.ds(t, 1), :] = row
    for s in range(scens):
        for t in range(2):
            pack_buf[s, pl.ds(t, 1), :] = grad_buf[pl.ds(t * scens + s, 1), :]
            noise_buf[s, pl.ds(t, 1), :] = noise_ref[0, t, pl.ds(s, 1), :]
    pack_in[place] = pack_buf[place]
    noise_in[place] = noise_buf[place]
    part_in[share] = part_buf[...]

    for fetch in fetches[8:]:
        fetch.wait()
    inputs = matrix_ref.shape[-1]
    matrix_high, matrix_low, _ = in_parts(matrix_ref[0])
    matrix_buf[:, 0:inputs] = matrix_high.astype(jnp.bfloat16)
    matrix_buf[:, inputs : 2 * inputs] = matrix_low.astype(jnp.bfloat16)

    pl.semaphore_wait(barrier, segments + sharers + areas - 3)

    def copy_to(axis, own, other, source, target, send, recv):
        return pltpu.make_async_remote_copy(
            src_ref=source,
            dst_ref=target.at[own],
            send_sem=send.at[other],
            recv_sem=recv.at[own],
            device_id={axis: other},
            device_id_type=pl.DeviceIdType.MESH,
        )

    def each(count, own, action):
        def body(k, carry):
            action(lax.rem(own + k, count))
            return carry

        lax.fori_loop(1, count, body, 0)

    partner = place + 1 - 2 * lax.rem(place, 2)

    def coef_copy(slot, other, sem):
        return pltpu.make_async_remote_copy(
            src_ref=coef_in.at[slot],
            dst_ref=coef_in.at[slot],
            send_sem=sem,
            recv_sem=coef_recv.at[slot],
            device_id={"hor": other},
            device_id_type=pl.DeviceIdType.MESH,
        )

    def each_chip(action):
        def body(k, carry):
            action(lax.rem(place + 2 * k, segments))
            return carry

        lax.fori_loop(1, segments // 2, body, 0)

    def part_copy(other):
        return copy_to("scen", share, other, part_buf, part_in, part_send, part_recv)

    def pack_copy(other):
        return copy_to("hor", place, other, pack_buf.at[other], pack_in, pack_send, pack_recv)

    def noise_copy(other):
        return copy_to("hor", place, other, noise_buf.at[other], noise_in, noise_send, noise_recv)

    def mean_copy(other):
        return copy_to("hor", place, other, mean_buf, mean_in, mean_send, mean_recv)

    def state_copy(other):
        return copy_to("hor", place, other, state_buf.at[other], state_in, state_send, state_recv)

    def boundary_copy(other):
        return copy_to(
            "area", area, other, boundary_buf, boundary_in, boundary_send, boundary_recv
        )

    def arrived(axis, other, source, target, send, recv):
        pltpu.make_async_remote_copy(
            src_ref=source,
            dst_ref=target.at[other],
            send_sem=send.at[other],
            recv_sem=recv.at[other],
            device_id={axis: other},
            device_id_type=pl.DeviceIdType.MESH,
        ).wait_recv()

    each(sharers, share, lambda o: part_copy(o).start())
    each_chip(lambda o: coef_copy(place, o, coef_send.at[o]).start())
    coef_copy(place, partner, pass_send.at[place]).start()
    each(segments, place, lambda o: pack_copy(o).start())
    each(
        sharers, share, lambda o: arrived("scen", o, part_buf, part_in, part_send, part_recv)
    )
    total = part_in[0]
    for k in range(1, sharers):
        total = total + part_in[k]
    mean_buf[...] = total * (1.0 / (scens * sharers))
    mean_in[place] = mean_buf[...]
    each(segments, place, lambda o: mean_copy(o).start())
    each(segments, place, lambda o: noise_copy(o).start())

    def relay(o):
        coef_copy(o, o, coef_send.at[o]).wait_recv()
        coef_copy(o, partner, pass_send.at[o]).start()

    each_chip(relay)
    coef_copy(partner, partner, pass_send.at[partner]).wait_recv()
    each_chip(
        lambda o: coef_copy(
            o + partner - place, partner, pass_send.at[o + partner - place]
        ).wait_recv()
    )

    first = lax.broadcasted_iota(jnp.int32, (8, extent), 0) == 0

    def wide(row):
        return jnp.broadcast_to(row, (8, extent))

    def back(k, costate):
        h = segments - 1 - k

        @pl.when(h != place)
        def _():
            arrived("hor", h, pack_buf.at[h], pack_in, pack_send, pack_recv)
            arrived("hor", h, mean_buf, mean_in, mean_send, mean_recv)

        for j in (1, 0):
            costate_buf[pl.ds(2 * h + j, 1), :] = costate[0:1, :]
            diag, up, down = (
                wide(coef_in[h, c, pl.ds(j, 1), :]) for c in range(3)
            )
            grad = jnp.where(
                first, wide(pack_in[h, pl.ds(j, 1), :]), wide(mean_in[h, pl.ds(j, 1), :])
            )
            if j == 0:
                costate_buf[pl.ds(2 * segments, 8), :] = costate
            costate = (
                (diag * costate + grad)
                + pltpu.roll(up * costate, STEP, 1)
                + pltpu.roll(down * costate, extent - STEP, 1)
            )
        return costate

    lax.fori_loop(0, segments, back, jnp.zeros((8, extent), jnp.float32))

    matrix_parts = matrix_buf[...]
    spread = picked(costate_buf[...], matrix_parts)
    controls = spread[:, 0:inputs] + spread[:, inputs : 2 * inputs]
    controls = -controls / penalty_ref[...]
    shared = controls[2 * segments + 1 : 2 * segments + 2, :]
    controls = controls[0 : 2 * segments, :]
    at_start = lax.broadcasted_iota(jnp.int32, controls.shape, 0) == 0
    controls = jnp.where(at_start, jnp.broadcast_to(shared, controls.shape), controls)
    count = 2 * segments
    parts = jnp.concatenate(in_parts(controls), axis=0).astype(jnp.bfloat16)
    force = lax.dot_general(
        jnp.concatenate([parts, parts], axis=1),
        matrix_parts,
        (((1,), (1,)), ((), ())),
        preferred_element_type=jnp.float32,
    )
    force_buf[...] = (force[0:count] + force[count : 2 * count]) + force[2 * count : 3 * count]
    each(
        segments,
        place,
        lambda o: arrived("hor", o, noise_buf.at[o], noise_in, noise_send, noise_recv),
    )

    def ahead_step(h, state):
        for j in (0, 1):
            state_buf[h, pl.ds(j, 1), :] = state[0:1, :]
            diag, up, down = (
                wide(coef_in[h, c, pl.ds(j, 1), :]) for c in range(3)
            )
            force = wide(force_buf[pl.ds(2 * h + j, 1), :] + noise_in[h, pl.ds(j, 1), :])
            state = (
                (diag * state + force)
                + up * pltpu.roll(state, extent - STEP, 1)
                + down * pltpu.roll(state, STEP, 1)
            )

        @pl.when(h != place)
        def _():
            state_copy(h).start()

        return state

    lax.fori_loop(0, segments, ahead_step, wide(start_ref[...]))
    state_in[place] = state_buf[place]
    each(
        segments,
        place,
        lambda o: arrived("hor", o, state_buf.at[o], state_in, state_send, state_recv),
    )
    for s in range(scens):
        for t in range(2):
            trajectory_ref[0, t, pl.ds(s, 1), :] = state_in[s, pl.ds(t, 1), :]
    put_state = pltpu.make_async_copy(trajectory_ref, trajectory_hbm, fetch_sem.at[0])
    put_state.start()
    narrow = selection.astype(jnp.bfloat16)
    for t in range(2):
        boundary_buf[t] = picked(trajectory_ref[0, t], narrow)
    each(areas, area, lambda o: boundary_copy(o).start())
    put_boundary = pltpu.make_async_copy(boundary_buf, boundary_in.at[area], fetch_sem.at[1])
    put_boundary.start()

    each(sharers, share, lambda o: part_copy(o).wait_send())

    def drain_chip(o):
        coef_copy(place, o, coef_send.at[o]).wait_send()
        coef_copy(o, partner, pass_send.at[o]).wait_send()

    each_chip(drain_chip)
    coef_copy(place, partner, pass_send.at[place]).wait_send()

    def drain(o):
        pack_copy(o).wait_send()
        mean_copy(o).wait_send()
        noise_copy(o).wait_send()
        state_copy(o).wait_send()

    each(segments, place, drain)
    each(areas, area, lambda o: boundary_copy(o).wait_send())
    put_state.wait()
    put_boundary.wait()
    each(
        areas,
        area,
        lambda o: arrived("area", o, boundary_buf, boundary_in, boundary_send, boundary_recv),
    )


def per_device(
    diagonal,
    band_coef,
    band_offsets,
    boundary_index,
    adjacency,
    start_state,
    input_matrix,
    input_penalty,
    linear_cost,
    disturbance,
    consensus,
    dual_values,
):
    segments = lax.axis_size("hor")
    sharers = lax.axis_size("scen")
    areas = lax.axis_size("area")
    extent = diagonal.shape[-1]
    anywhere = pl.BlockSpec(memory_space=pl.ANY)
    real = jnp.float32
    scratch = [
        pltpu.SMEM(band_offsets.shape, jnp.int32),
    ]
    scratch += [
        pltpu.VMEM(held.shape, held.dtype)
        for held in (
            diagonal,
            band_coef,
            boundary_index,
            start_state,
            input_matrix,
            input_penalty,
            linear_cost,
            disturbance,
            consensus,
            dual_values,
            linear_cost,
        )
    ]
    scratch += [
        pltpu.VMEM((2 * segments, extent), real),
        pltpu.VMEM((segments, 3, 2, extent), real),
        pltpu.VMEM((segments, 2, extent), real),
        pltpu.VMEM((segments, 2, extent), real),
        pltpu.VMEM((segments, 2, extent), real),
        pltpu.VMEM((segments, 2, extent), real),
        pltpu.VMEM((2, extent), real),
        pltpu.VMEM((sharers, 2, extent), real),
        pltpu.VMEM((2, extent), real),
        pltpu.VMEM((segments, 2, extent), real),
        pltpu.VMEM((2 * segments + 8, extent), real),
        pltpu.VMEM((2 * segments, extent), real),
        pltpu.VMEM((segments, 2, extent), real),
        pltpu.VMEM((segments, 2, extent), real),
        pltpu.VMEM(dual_values.shape[1:], real),
        pltpu.VMEM((extent, 2 * input_matrix.shape[-1]), jnp.bfloat16),
    ]
    scratch += [pltpu.SemaphoreType.DMA((12,))]
    scratch += [pltpu.SemaphoreType.DMA((segments,)) for _ in range(3)]
    for count in (segments, segments, sharers, segments, segments, areas):
        scratch += [pltpu.SemaphoreType.DMA((count,)), pltpu.SemaphoreType.DMA((count,))]
    states, boundaries = pl.pallas_call(
        functools.partial(kernel, segments, sharers, areas),
        out_shape=(
            jax.ShapeDtypeStruct(linear_cost.shape, real),
            jax.ShapeDtypeStruct((areas, *dual_values.shape[1:]), real),
        ),
        in_specs=[anywhere] * 11,
        out_specs=(anywhere,) * 2,
        scratch_shapes=scratch,
        compiler_params=pltpu.CompilerParams(collective_id=0, has_side_effects=True),
    )(
        band_offsets,
        diagonal,
        band_coef,
        boundary_index,
        start_state,
        input_matrix,
        input_penalty,
        linear_cost,
        disturbance,
        consensus,
        dual_values,
    )
    vmem = pl.BlockSpec(memory_space=pltpu.VMEM)
    return pl.pallas_call(
        finish,
        out_shape=(
            jax.ShapeDtypeStruct(linear_cost.shape, real),
            jax.ShapeDtypeStruct(dual_values.shape, real),
            jax.ShapeDtypeStruct(dual_values.shape, real),
        ),
        in_specs=[pl.BlockSpec(memory_space=pltpu.SMEM)] + [vmem] * 3,
        out_specs=(vmem,) * 3,
    )(adjacency, dual_values, states, boundaries)


def solution(mesh):
    in_specs = (
        P("area", "hor", None),
        P("area", "hor", None, None),
        P("area", None),
        P("area", None),
        P("area", None),
        P("area", None),
        P("area", None, None),
        P("area", None),
        P("area", "hor", "scen", None),
        P("area", "hor", "scen", None),
        P("area", "hor", "scen", None),
        P("area", "hor", "scen", None),
    )
    out_specs = (
        P("area", "hor", "scen", None),
        P("area", "hor", "scen", None),
        P("area", "hor", "scen", None),
    )
    return jax.shard_map(
        per_device, mesh=mesh, in_specs=in_specs, out_specs=out_specs, check_vma=False
    )
```

```python
import functools

import jax
import jax.numpy as jnp
from jax import lax
from jax.experimental import pallas as pl
from jax.experimental.pallas import tpu as pltpu
from jax.sharding import PartitionSpec as P

STEP = 16
NNB = 3

highest = lax.Precision.HIGHEST


def product(left, right):
    return jnp.dot(left, right, precision=highest, preferred_element_type=jnp.float32)


def product_transposed(left, right):
    return lax.dot_general(
        left, right, (((1,), (1,)), ((), ())), precision=highest, preferred_element_type=jnp.float32
    )


def in_parts(rows):
    high = rows.astype(jnp.bfloat16).astype(jnp.float32)
    middle = (rows - high).astype(jnp.bfloat16).astype(jnp.float32)
    return high, middle, (rows - high) - middle


def picked(rows, selection):
    count = rows.shape[0]
    parts = list(in_parts(rows))
    if 3 * count % 16:
        parts.append(jnp.zeros((16 - 3 * count % 16, rows.shape[1]), jnp.float32))
    parts = jnp.concatenate(parts, axis=0).astype(jnp.bfloat16)
    out = jnp.dot(parts, selection, preferred_element_type=jnp.float32)
    return (out[0:count] + out[count : 2 * count]) + out[2 * count : 3 * count]


def finish(
    adjacency_ref, dual_ref, state_ref, boundary_ref, trajectory_ref, agreed_ref, updated_ref
):
    area = lax.axis_index("area")
    own = boundary_ref[area]
    summed = own
    for n in range(boundary_ref.shape[0]):
        weight = jnp.float32(0.0)
        for j in range(NNB):
            weight = weight + jnp.where(adjacency_ref[0, j] == n, 1.0, 0.0)
        summed = summed + weight * boundary_ref[n]
    agreed = summed * (1.0 / (NNB + 1))
    trajectory_ref[...] = state_ref[...]
    agreed_ref[0] = agreed
    updated_ref[0] = dual_ref[0] + own - agreed


def kernel(
    segments,
    sharers,
    areas,
    offsets_hbm,
    diagonal_hbm,
    band_hbm,
    index_hbm,
    start_hbm,
    matrix_hbm,
    penalty_hbm,
    cost_hbm,
    noise_hbm,
    consensus_hbm,
    dual_hbm,
    trajectory_hbm,
    boundary_in,
    offsets_ref,
    diagonal_ref,
    band_ref,
    index_ref,
    start_ref,
    matrix_ref,
    penalty_ref,
    cost_ref,
    noise_ref,
    consensus_ref,
    dual_ref,
    trajectory_ref,
    grad_buf,
    coef_in,
    pack_buf,
    pack_in,
    noise_buf,
    noise_in,
    part_buf,
    part_in,
    mean_buf,
    mean_in,
    costate_buf,
    force_buf,
    state_buf,
    state_in,
    boundary_buf,
    matrix_buf,
    fetch_sem,
    coef_send,
    pass_send,
    coef_recv,
    pack_send,
    pack_recv,
    noise_send,
    noise_recv,
    part_send,
    part_recv,
    mean_send,
    mean_recv,
    state_send,
    state_recv,
    boundary_send,
    boundary_recv,
):
    place = lax.axis_index("hor")
    share = lax.axis_index("scen")
    area = lax.axis_index("area")
    scens = segments
    extent = diagonal_ref.shape[-1]

    barrier = pltpu.get_barrier_semaphore()

    def greet(axis, own, count):
        def body(k, carry):
            pl.semaphore_signal(
                barrier,
                inc=1,
                device_id={axis: lax.rem(own + k, count)},
                device_id_type=pl.DeviceIdType.MESH,
            )
            return carry

        lax.fori_loop(1, count, body, 0)

    greet("hor", place, segments)
    greet("scen", share, sharers)
    greet("area", area, areas)

    fetches = [
        pltpu.make_async_copy(source, target, fetch_sem.at[k])
        for k, (source, target) in enumerate(
            (
                (offsets_hbm, offsets_ref),
                (band_hbm, band_ref),
                (diagonal_hbm, diagonal_ref),
                (index_hbm, index_ref),
                (dual_hbm, dual_ref),
                (consensus_hbm, consensus_ref),
                (cost_hbm, cost_ref),
                (noise_hbm, noise_ref),
                (matrix_hbm, matrix_ref),
                (penalty_hbm, penalty_ref),
                (start_hbm, start_ref),
            )
        )
    ]
    for fetch in fetches:
        fetch.start()
    for fetch in fetches[:8]:
        fetch.wait()

    selection = (
        lax.broadcasted_iota(jnp.int32, (extent, index_ref.shape[-1]), 0) == index_ref[...]
    ).astype(jnp.float32)
    for t in range(2):
        grad_buf[pl.ds(t * scens, scens), :] = cost_ref[0, t] + product_transposed(
            dual_ref[0, t] - consensus_ref[0, t], selection
        )
        part_buf[pl.ds(t, 1), :] = jnp.sum(
            grad_buf[pl.ds(t * scens, scens), :], axis=0, keepdims=True
        )
    lane = lax.broadcasted_iota(jnp.int32, (1, extent), 1)
    for t in range(2):
        up = jnp.zeros((1, extent), jnp.float32)
        down = jnp.zeros((1, extent), jnp.float32)
        for b in range(band_ref.shape[2]):
            coef = band_ref[0, t, pl.ds(b, 1), :]
            ahead = jnp.where(offsets_ref[0, b] > 0, 1.0, 0.0)
            up = up + ahead * coef
            down = down + (1.0 - ahead) * coef
        up = jnp.where(lane >= extent - STEP, 0.0, up)
        down = jnp.where(lane < STEP, 0.0, down)
        for c, row in enumerate((diagonal_ref[0, pl.ds(t, 1), :], up, down)):
            coef_in[place, c, pl.ds(t, 1), :] = row
    for s in range(scens):
        for t in range(2):
            pack_buf[s, pl.ds(t, 1), :] = grad_buf[pl.ds(t * scens + s, 1), :]
            noise_buf[s, pl.ds(t, 1), :] = noise_ref[0, t, pl.ds(s, 1), :]
    pack_in[place] = pack_buf[place]
    noise_in[place] = noise_buf[place]
    part_in[share] = part_buf[...]

    for fetch in fetches[8:]:
        fetch.wait()
    inputs = matrix_ref.shape[-1]
    matrix_high, matrix_low, _ = in_parts(matrix_ref[0])
    matrix_buf[:, 0:inputs] = matrix_high.astype(jnp.bfloat16)
    matrix_buf[:, inputs : 2 * inputs] = matrix_low.astype(jnp.bfloat16)

    pl.semaphore_wait(barrier, segments + sharers + areas - 3)

    def copy_to(axis, own, other, source, target, send, recv):
        return pltpu.make_async_remote_copy(
            src_ref=source,
            dst_ref=target.at[own],
            send_sem=send.at[other],
            recv_sem=recv.at[own],
            device_id={axis: other},
            device_id_type=pl.DeviceIdType.MESH,
        )

    def each(count, own, action):
        def body(k, carry):
            action(lax.rem(own + k, count))
            return carry

        lax.fori_loop(1, count, body, 0)

    partner = place + 1 - 2 * lax.rem(place, 2)

    def coef_copy(slot, other, sem):
        return pltpu.make_async_remote_copy(
            src_ref=coef_in.at[slot],
            dst_ref=coef_in.at[slot],
            send_sem=sem,
            recv_sem=coef_recv.at[slot],
            device_id={"hor": other},
            device_id_type=pl.DeviceIdType.MESH,
        )

    def each_chip(action):
        def body(k, carry):
            action(lax.rem(place + 2 * k, segments))
            return carry

        lax.fori_loop(1, segments // 2, body, 0)

    def part_copy(other):
        return copy_to("scen", share, other, part_buf, part_in, part_send, part_recv)

    def pack_copy(other):
        return copy_to("hor", place, other, pack_buf.at[other], pack_in, pack_send, pack_recv)

    def noise_copy(other):
        return copy_to("hor", place, other, noise_buf.at[other], noise_in, noise_send, noise_recv)

    def mean_copy(other):
        return copy_to("hor", place, other, mean_buf, mean_in, mean_send, mean_recv)

    def state_copy(other):
        return copy_to("hor", place, other, state_buf.at[other], state_in, state_send, state_recv)

    def boundary_copy(t, other, own):
        return pltpu.make_async_remote_copy(
            src_ref=boundary_buf.at[t],
            dst_ref=boundary_in.at[own, t],
            send_sem=boundary_send.at[t, other],
            recv_sem=boundary_recv.at[t, own],
            device_id={"area": other},
            device_id_type=pl.DeviceIdType.MESH,
        )

    def arrived(axis, other, source, target, send, recv):
        pltpu.make_async_remote_copy(
            src_ref=source,
            dst_ref=target.at[other],
            send_sem=send.at[other],
            recv_sem=recv.at[other],
            device_id={axis: other},
            device_id_type=pl.DeviceIdType.MESH,
        ).wait_recv()

    each(sharers, share, lambda o: part_copy(o).start())
    each_chip(lambda o: coef_copy(place, o, coef_send.at[o]).start())
    coef_copy(place, partner, pass_send.at[place]).start()
    each(segments, place, lambda o: pack_copy(o).start())
    each(
        sharers, share, lambda o: arrived("scen", o, part_buf, part_in, part_send, part_recv)
    )
    total = part_in[0]
    for k in range(1, sharers):
        total = total + part_in[k]
    mean_buf[...] = total * (1.0 / (scens * sharers))
    mean_in[place] = mean_buf[...]
    each(segments, place, lambda o: mean_copy(o).start())
    each(segments, place, lambda o: noise_copy(o).start())

    def relay(o):
        coef_copy(o, o, coef_send.at[o]).wait_recv()
        coef_copy(o, partner, pass_send.at[o]).start()

    each_chip(relay)
    coef_copy(partner, partner, pass_send.at[partner]).wait_recv()
    each_chip(
        lambda o: coef_copy(
            o + partner - place, partner, pass_send.at[o + partner - place]
        ).wait_recv()
    )

    first = lax.broadcasted_iota(jnp.int32, (8, extent), 0) == 0

    def wide(row):
        return jnp.broadcast_to(row, (8, extent))

    def back(k, costate):
        h = segments - 1 - k

        @pl.when(h != place)
        def _():
            arrived("hor", h, pack_buf.at[h], pack_in, pack_send, pack_recv)
            arrived("hor", h, mean_buf, mean_in, mean_send, mean_recv)

        for j in (1, 0):
            costate_buf[pl.ds(2 * h + j, 1), :] = costate[0:1, :]
            diag, up, down = (
                wide(coef_in[h, c, pl.ds(j, 1), :]) for c in range(3)
            )
            grad = jnp.where(
                first, wide(pack_in[h, pl.ds(j, 1), :]), wide(mean_in[h, pl.ds(j, 1), :])
            )
            if j == 0:
                costate_buf[pl.ds(2 * segments, 8), :] = costate
            costate = (
                (diag * costate + grad)
                + pltpu.roll(up * costate, STEP, 1)
                + pltpu.roll(down * costate, extent - STEP, 1)
            )
        return costate

    lax.fori_loop(0, segments, back, jnp.zeros((8, extent), jnp.float32))

    matrix_parts = matrix_buf[...]
    spread = picked(costate_buf[...], matrix_parts)
    controls = spread[:, 0:inputs] + spread[:, inputs : 2 * inputs]
    controls = -controls / penalty_ref[...]
    shared = controls[2 * segments + 1 : 2 * segments + 2, :]
    controls = controls[0 : 2 * segments, :]
    at_start = lax.broadcasted_iota(jnp.int32, controls.shape, 0) == 0
    controls = jnp.where(at_start, jnp.broadcast_to(shared, controls.shape), controls)
    count = 2 * segments
    parts = jnp.concatenate(in_parts(controls), axis=0).astype(jnp.bfloat16)
    force = lax.dot_general(
        jnp.concatenate([parts, parts], axis=1),
        matrix_parts,
        (((1,), (1,)), ((), ())),
        preferred_element_type=jnp.float32,
    )
    force_buf[...] = (force[0:count] + force[count : 2 * count]) + force[2 * count : 3 * count]
    each(
        segments,
        place,
        lambda o: arrived("hor", o, noise_buf.at[o], noise_in, noise_send, noise_recv),
    )

    def ahead_step(h, state):
        for j in (0, 1):
            state_buf[h, pl.ds(j, 1), :] = state[0:1, :]
            diag, up, down = (
                wide(coef_in[h, c, pl.ds(j, 1), :]) for c in range(3)
            )
            force = wide(force_buf[pl.ds(2 * h + j, 1), :] + noise_in[h, pl.ds(j, 1), :])
            state = (
                (diag * state + force)
                + up * pltpu.roll(state, extent - STEP, 1)
                + down * pltpu.roll(state, STEP, 1)
            )

        @pl.when(h != place)
        def _():
            state_copy(h).start()

        return state

    lax.fori_loop(0, segments, ahead_step, wide(start_ref[...]))
    state_in[place] = state_buf[place]
    for s in range(scens):

        @pl.when(s != place)
        def _(s=s):
            arrived("hor", s, state_buf.at[s], state_in, state_send, state_recv)

        for t in range(2):
            trajectory_ref[0, t, pl.ds(s, 1), :] = state_in[s, pl.ds(t, 1), :]
    put_state = pltpu.make_async_copy(trajectory_ref, trajectory_hbm, fetch_sem.at[0])
    put_state.start()
    narrow = selection.astype(jnp.bfloat16)
    for t in range(2):
        boundary_buf[t] = picked(trajectory_ref[0, t], narrow)
        each(areas, area, lambda o, t=t: boundary_copy(t, o, area).start())
    put_boundary = pltpu.make_async_copy(boundary_buf, boundary_in.at[area], fetch_sem.at[1])
    put_boundary.start()

    each(sharers, share, lambda o: part_copy(o).wait_send())

    def drain_chip(o):
        coef_copy(place, o, coef_send.at[o]).wait_send()
        coef_copy(o, partner, pass_send.at[o]).wait_send()

    each_chip(drain_chip)
    coef_copy(place, partner, pass_send.at[place]).wait_send()

    def drain(o):
        pack_copy(o).wait_send()
        mean_copy(o).wait_send()
        noise_copy(o).wait_send()
        state_copy(o).wait_send()

    each(segments, place, drain)
    for t in range(2):
        each(areas, area, lambda o, t=t: boundary_copy(t, o, area).wait_send())
    put_state.wait()
    put_boundary.wait()
    for t in range(2):
        each(areas, area, lambda o, t=t: boundary_copy(t, o, o).wait_recv())


def per_device(
    diagonal,
    band_coef,
    band_offsets,
    boundary_index,
    adjacency,
    start_state,
    input_matrix,
    input_penalty,
    linear_cost,
    disturbance,
    consensus,
    dual_values,
):
    segments = lax.axis_size("hor")
    sharers = lax.axis_size("scen")
    areas = lax.axis_size("area")
    extent = diagonal.shape[-1]
    anywhere = pl.BlockSpec(memory_space=pl.ANY)
    real = jnp.float32
    scratch = [
        pltpu.SMEM(band_offsets.shape, jnp.int32),
    ]
    scratch += [
        pltpu.VMEM(held.shape, held.dtype)
        for held in (
            diagonal,
            band_coef,
            boundary_index,
            start_state,
            input_matrix,
            input_penalty,
            linear_cost,
            disturbance,
            consensus,
            dual_values,
            linear_cost,
        )
    ]
    scratch += [
        pltpu.VMEM((2 * segments, extent), real),
        pltpu.VMEM((segments, 3, 2, extent), real),
        pltpu.VMEM((segments, 2, extent), real),
        pltpu.VMEM((segments, 2, extent), real),
        pltpu.VMEM((segments, 2, extent), real),
        pltpu.VMEM((segments, 2, extent), real),
        pltpu.VMEM((2, extent), real),
        pltpu.VMEM((sharers, 2, extent), real),
        pltpu.VMEM((2, extent), real),
        pltpu.VMEM((segments, 2, extent), real),
        pltpu.VMEM((2 * segments + 8, extent), real),
        pltpu.VMEM((2 * segments, extent), real),
        pltpu.VMEM((segments, 2, extent), real),
        pltpu.VMEM((segments, 2, extent), real),
        pltpu.VMEM(dual_values.shape[1:], real),
        pltpu.VMEM((extent, 2 * input_matrix.shape[-1]), jnp.bfloat16),
    ]
    scratch += [pltpu.SemaphoreType.DMA((12,))]
    scratch += [pltpu.SemaphoreType.DMA((segments,)) for _ in range(3)]
    for count in (segments, segments, sharers, segments, segments):
        scratch += [pltpu.SemaphoreType.DMA((count,)), pltpu.SemaphoreType.DMA((count,))]
    scratch += [pltpu.SemaphoreType.DMA((2, areas)) for _ in range(2)]
    states, boundaries = pl.pallas_call(
        functools.partial(kernel, segments, sharers, areas),
        out_shape=(
            jax.ShapeDtypeStruct(linear_cost.shape, real),
            jax.ShapeDtypeStruct((areas, *dual_values.shape[1:]), real),
        ),
        in_specs=[anywhere] * 11,
        out_specs=(anywhere,) * 2,
        scratch_shapes=scratch,
        compiler_params=pltpu.CompilerParams(collective_id=0, has_side_effects=True),
    )(
        band_offsets,
        diagonal,
        band_coef,
        boundary_index,
        start_state,
        input_matrix,
        input_penalty,
        linear_cost,
        disturbance,
        consensus,
        dual_values,
    )
    vmem = pl.BlockSpec(memory_space=pltpu.VMEM)
    return pl.pallas_call(
        finish,
        out_shape=(
            jax.ShapeDtypeStruct(linear_cost.shape, real),
            jax.ShapeDtypeStruct(dual_values.shape, real),
            jax.ShapeDtypeStruct(dual_values.shape, real),
        ),
        in_specs=[pl.BlockSpec(memory_space=pltpu.SMEM)] + [vmem] * 3,
        out_specs=(vmem,) * 3,
    )(adjacency, dual_values, states, boundaries)


def solution(mesh):
    in_specs = (
        P("area", "hor", None),
        P("area", "hor", None, None),
        P("area", None),
        P("area", None),
        P("area", None),
        P("area", None),
        P("area", None, None),
        P("area", None),
        P("area", "hor", "scen", None),
        P("area", "hor", "scen", None),
        P("area", "hor", "scen", None),
        P("area", "hor", "scen", None),
    )
    out_specs = (
        P("area", "hor", "scen", None),
        P("area", "hor", "scen", None),
        P("area", "hor", "scen", None),
    )
    return jax.shard_map(
        per_device, mesh=mesh, in_specs=in_specs, out_specs=out_specs, check_vma=False
    )
```
